128 devices in a mesh: tm: 4 (over x), row: 32 (over z, y, core).
Axes of the slice: x: 4, y: 4, z: 4, core: 2. Of those that a mesh axis runs over, the one named last changes fastest.
Arguments:
- coupling: float32 [4, 8192, 8192], P('tm', 'row'), may hold values from -0.0625 to 0.0625
- damping: float32 [4, 8192], P('tm', 'row'), may hold values from 0.5 to 3
- forcing: float32 [4, 8, 8192], P('tm', None, 'row'), may hold values from -6 to 6
- initial: float32 [8, 8192], P(None, 'row'), may hold values from -6 to 6
- counts: int32 [4], P('tm'), may hold values from 1 to 8
Outputs:
- states: float32 [4, 8, 8192], P('tm', None, 'row')
The draws below stay inside these ranges and needn't reach their ends.
All inputs are finite; a program needn't handle non-finite values.
Results may differ from the reference program's by a relative error of at most 0.00013.
Values sent between devices are 32-bit elements; how exact they have to be, the bound alone decides.
A program may use at most 64 MiB of HBM per device.

```python
import math
import jax
import jax.numpy as jnp
from jax import lax

N = 8192
KRYLOV = 2
MEMBERS = 8
SLABS = 4


def plant(values, key, smallest, high):
    spot = [jax.random.randint(jax.random.fold_in(key, axis), (), 0, length) for axis, length in enumerate(values.shape)]
    main_axis = values.shape.index(max(values.shape))
    beside = spot[:main_axis] + [(spot[main_axis] + 1) % values.shape[main_axis]] + spot[main_axis + 1:]
    return values.at[tuple(spot)].set(smallest).at[tuple(beside)].set(high)


def levels(rng, shape, cuts, least, top_value):
    loudness, own = 1.0, jax.random.fold_in(rng, 6)
    for axis_at, blocks in cuts:
        steps = jnp.exp(jax.random.uniform(jax.random.fold_in(own, axis_at), (blocks,), jnp.float32, least / len(cuts), top_value / len(cuts)))
        loudness = loudness * jnp.repeat(steps, shape[axis_at] // blocks).reshape([-1 if axis == axis_at else 1 for axis in range(len(shape))])
    return loudness


def scatter_about(own_key, shape, scale, reach, cuts=(), kind=jnp.bfloat16):
    values = scale * jax.random.normal(own_key, shape, jnp.float32)
    if cuts:
        values = values * levels(own_key, shape, cuts, -0.22, 0.18)
    return jnp.clip(values, -reach, reach).astype(kind)


def setup_inputs(seed: int = 0) -> dict:
    splits = jax.random.split(jax.random.key(seed), 6)
    return {
        "coupling": scatter_about(splits[0], (SLABS, N, N), N ** -0.5, 0.0625, ((0, 4), (1, 32)), jnp.float32),
        "damping": jnp.clip(jnp.exp(math.log(3.0) - 1.7917595 * jax.random.uniform(splits[1], (SLABS, N), jnp.float32) ** levels(splits[1], (SLABS, N), ((0, 4), (1, 32)), -0.2, 0.2)), 0.5, 3.0),
        "forcing": scatter_about(splits[2], (SLABS, MEMBERS, N), 1.0, 6.0, ((0, 4), (2, 32)), jnp.float32),
        "initial": scatter_about(splits[3], (MEMBERS, N), 1.0, 6.0, ((1, 32),), jnp.float32),
        "counts": plant(jax.random.randint(splits[4], (SLABS,), 1, 9), jax.random.fold_in(splits[4], 1), 1, 8).astype(jnp.int32),
    }


time_step = 0.125
epsilon = 1e-06
squarings = 5
taylor_terms = 12
highest = lax.Precision.HIGHEST

def matrix_exponential(matrix):
    scaled = matrix / 2.0 ** squarings
    dimension = matrix.shape[-1]
    identity = jnp.broadcast_to(jnp.eye(dimension, dtype=jnp.float32), matrix.shape)
    result = identity
    for degree in range(taylor_terms, 0, -1):
        result = identity + jnp.einsum('bij,bjk->bik', scaled, result, precision=highest) / degree
    for repeat in range(squarings):
        result = jnp.einsum('bij,bjk->bik', result, result, precision=highest)
    return result

def exponent_block(hessenberg, step_size):
    members = hessenberg.shape[0]
    augmented = jnp.zeros((members, KRYLOV + 1, KRYLOV + 1), jnp.float32)
    augmented = augmented.at[:, :KRYLOV, :KRYLOV].set(step_size * hessenberg)
    augmented = augmented.at[:, 0, KRYLOV].set(1.0)
    return matrix_exponential(augmented)

def apply_operator(vectors, coupling, damping):
    product = lax.dot_general(vectors, coupling, (((1,), (1,)), ((), ())), precision=highest, preferred_element_type=jnp.float32)
    return product - damping * vectors

def arnoldi(vectors, coupling, damping):
    members = vectors.shape[0]
    extent = vectors.shape[1]
    start_norm = jnp.sqrt(lax.optimization_barrier(jnp.sum(vectors * vectors, axis=1)) + epsilon)
    krylov_basis = jnp.zeros((KRYLOV, members, extent), jnp.float32).at[0].set(vectors / start_norm[:, None])
    hessenberg = jnp.zeros((members, KRYLOV, KRYLOV), jnp.float32)
    for column in range(KRYLOV):
        applied = apply_operator(krylov_basis[column], coupling, damping)
        weights = jnp.einsum('kbn,bn->kb', krylov_basis, applied, precision=highest)
        applied = applied - jnp.einsum('kb,kbn->bn', weights, krylov_basis, precision=highest)
        hessenberg = hessenberg.at[:, :, column].set(weights.T)
        if column + 1 < KRYLOV:
            length = jnp.sqrt(lax.optimization_barrier(jnp.sum(applied * applied, axis=1)) + epsilon)
            krylov_basis = krylov_basis.at[column + 1].set(applied / length[:, None])
            hessenberg = hessenberg.at[:, column + 1, column].set(length)
    return (start_norm, krylov_basis, hessenberg)

def combine_basis(krylov_basis, coefficients):
    return jnp.einsum('kbn,bk->bn', krylov_basis, coefficients, precision=highest)

def reference(coupling, damping, forcing, initial, counts):
    states = []
    carried = initial
    for slab_index in range(SLABS):
        step_size = counts[slab_index].astype(jnp.float32) * time_step
        forcing_norm, forcing_basis, forcing_hessenberg = arnoldi(forcing[slab_index], coupling[slab_index], damping[slab_index])
        forcing_block = exponent_block(forcing_hessenberg, step_size)
        local_part = combine_basis(forcing_basis, (step_size * forcing_norm)[:, None] * forcing_block[:, :KRYLOV, KRYLOV])
        carried_norm, carried_basis, carried_hessenberg = arnoldi(carried, coupling[slab_index], damping[slab_index])
        carried_block = exponent_block(carried_hessenberg, step_size)
        carried = combine_basis(carried_basis, carried_norm[:, None] * carried_block[:, :KRYLOV, 0]) + local_part
        states.append(carried)
    return jnp.stack(states)
```

```python
import functools

import jax
import jax.numpy as jnp
from jax import lax
from jax.experimental import pallas as pl
from jax.experimental.pallas import tpu as pltpu
from jax.sharding import PartitionSpec as P

MESH = pl.DeviceIdType.MESH
TIME_STEP = 0.125
EPSILON = 1e-06
SQUARINGS = 5
TAYLOR_TERMS = 12
SIDE = 4
LANES = 128
CHUNKS = 8


def offset(i):
    return lax.rem(2 + i + i // 2 + 2 * (i // 3), SIDE)


def exponential(h, g, below, above, corner):
    scale = h * (1.0 / 2.0**SQUARINGS)
    s00, s01, s10, s11 = g * scale, above * scale, below * scale, corner * scale
    edge = 1.0 / 2.0**SQUARINGS
    one, zero = jnp.ones_like(s00), jnp.zeros_like(s00)
    r00, r01, r10, r11, c0, c1 = one, zero, zero, one, zero, zero
    for degree in range(TAYLOR_TERMS, 0, -1):
        f = 1.0 / degree
        r00, r01, r10, r11, c0, c1 = (
            1.0 + (s00 * r00 + s01 * r10) * f,
            (s00 * r01 + s01 * r11) * f,
            (s10 * r00 + s11 * r10) * f,
            1.0 + (s10 * r01 + s11 * r11) * f,
            (s00 * c0 + s01 * c1 + edge) * f,
            (s10 * c0 + s11 * c1) * f,
        )
    for _ in range(SQUARINGS):
        r00, r01, r10, r11, c0, c1 = (
            r00 * r00 + r01 * r10,
            r00 * r01 + r01 * r11,
            r10 * r00 + r11 * r10,
            r10 * r01 + r11 * r11,
            r00 * c0 + r01 * c1 + c0,
            r10 * c0 + r11 * c1 + c1,
        )
    return r00, r10, c0, c1


def kernel(
    members, rows, parts, slabs,
    a_hbm, damp_ref, f_ref, c_ref, n_ref, o_ref,
    stage, at, xs, g0, gf, gu, lb, pr, ck, tb, tf, tp, ls, prs,
    a_sem, send, recv,
):
    t, r = lax.axis_index("tm"), lax.axis_index("row")
    core, chip = lax.rem(r, 2), r // 2
    z, y = chip // SIDE, lax.rem(chip, SIDE)
    width = a_hbm.shape[2] // CHUNKS
    G0, GF, GU, LBR, LB, PRR, PR, TF, TB, TP = range(10)

    def loads(j):
        return pltpu.make_async_copy(
            a_hbm.at[0, :, pl.ds(j * width, width)], stage.at[j], a_sem.at[j]
        )

    def copy(src, dst, k, device):
        return pltpu.make_async_remote_copy(
            src_ref=src, dst_ref=dst, send_sem=send.at[k], recv_sem=recv.at[k],
            device_id=device, device_id_type=MESH,
        )

    def other(i):
        zz, yy = lax.rem(z + offset(i // SIDE), SIDE), lax.rem(y + offset(lax.rem(i, SIDE)), SIDE)
        return 2 * (zz * SIDE + yy)

    def spread(src, dst, k):
        @pl.loop(0, parts // 2 - 1)
        def _(i):
            at_chip = other(i)
            copy(src, dst, k, (t, at_chip + core)).start()
            copy(src, dst, k, (t, at_chip + 1 - core)).start()

        copy(src, dst, k, (t, chip * 2 + 1 - core)).start()

    def spread_next(src, dst, k):
        @pl.loop(0, parts // 2)
        def _(i):
            at_chip = other(i)
            copy(src, dst, k, (t + 1, at_chip + core)).start()
            copy(src, dst, k, (t + 1, at_chip + 1 - core)).start()

    def arrived(buffer, k, count=parts - 1):
        some = buffer.at[pl.ds(0, count)]
        pltpu.make_async_copy(some, some, recv.at[k]).wait()

    def left(buffer, k, count=parts - 1):
        some = buffer.at[pl.ds(0, count)]
        pltpu.make_async_copy(some, some, send.at[k]).wait()

    def fill(slot, at_part, v):
        high = v.astype(jnp.bfloat16).astype(jnp.float32)
        both = jnp.concatenate([high, v - high], axis=0).astype(jnp.bfloat16)
        xs[16 * slot : 16 * slot + 16, rows * at_part : rows * at_part + rows] = both

    def product(count):
        d = jnp.dot(xs[0 : 16 * count, :], at[...], preferred_element_type=jnp.float32)
        out = []
        for j in range(count):
            top, low = d[16 * j : 16 * j + 8], d[16 * j + 8 : 16 * j + 16]
            out.append(top[:, :rows] + (top[:, rows:] + low[:, :rows]))
        return out

    damp = damp_ref[...]

    def moments(first, second):
        n2 = jnp.zeros((members, rows), jnp.float32)
        d = jnp.zeros((members, rows), jnp.float32)
        for p in range(parts):
            c = first(p)
            n2 += c * c
            d += c * second(p)
        b2 = jnp.sum(n2, axis=1, keepdims=True) + EPSILON
        return b2, jnp.sum(d, axis=1, keepdims=True) / b2

    def remainder(first, second, g, keep):
        w2 = jnp.zeros((members, rows), jnp.float32)
        for p in range(parts):
            w = second(p) - g * first(p)
            if keep:
                fill(0, p, w)
            w2 += w * w
        return jnp.sum(w2, axis=1, keepdims=True)

    def second_step(first, second, own_first, own_second):
        b2, g = moments(first, second)
        below = jnp.sqrt(remainder(first, second, g, True) / b2 + EPSILON)
        w = own_second - g * own_first
        image = product(1)[0] - damp * w
        t0 = jnp.sum(own_first * image, axis=1, keepdims=True)
        t1 = jnp.sum(w * image, axis=1, keepdims=True)
        return (b2, g, below), (t0, t1)

    lane = lax.broadcasted_iota(jnp.int32, (members, LANES), 1)
    member = lax.broadcasted_iota(jnp.int32, (members, LANES), 0)

    def packed(columns):
        row = jnp.zeros((members, LANES), jnp.float32)
        for j, column in enumerate(columns):
            if column is not None:
                row = jnp.where(lane == member + members * j, column, row)
        return jnp.sum(row, axis=0, keepdims=True)

    def unpacked(buffer, count):
        total = jnp.sum(buffer[...], axis=0)
        total = jnp.broadcast_to(total, (members, LANES))
        return [
            jnp.sum(jnp.where(lane == member + members * j, total, 0.0), axis=1, keepdims=True)
            for j in range(count)
        ]

    def start_weights(h, known, t0, t1):
        b2, g, below = known
        e00, e10, _, _ = exponential(h, g, below, t0 / (b2 * below), t1 / (b2 * below * below))
        x2 = e10 / below
        return e00 - g * x2, x2

    def forcing_weights(h, known, t0, t1):
        b2, g, below = known
        _, _, c0, c1 = exponential(h, g, below, t0 / (b2 * below), t1 / (b2 * below * below))
        x4 = h * c1 / below
        return h * c0 - g * x4, x4

    for j in range(CHUNKS):
        loads(j).start()
    barrier = pltpu.get_barrier_semaphore()

    @pl.loop(1, parts)
    def _(k):
        pl.semaphore_signal(
            barrier, inc=1, device_id=(t, lax.rem(r + k, parts)), device_id_type=MESH
        )

    for by in (1, -1):

        @pl.when(t + 1 < slabs if by == 1 else t > 0)
        def _():
            @pl.loop(0, parts)
            def _(k):
                pl.semaphore_signal(
                    barrier, inc=1, device_id=(t + by, lax.rem(r + k, parts)), device_id_type=MESH
                )

    h = jnp.full((members, 1), n_ref[0].astype(jnp.float32) * TIME_STEP, jnp.float32)
    g0[r] = jnp.concatenate([f_ref[...], c_ref[...]], axis=0)
    pl.semaphore_wait(barrier, parts - 1 + parts * (jnp.minimum(t, 1) + jnp.minimum(slabs - 1 - t, 1)))

    spread(g0.at[r], g0.at[r], G0)

    @pl.when(t == 0)
    def _():
        ls[...] = f_ref[...]
        copy(ls, lb.at[r], LBR, (t + 1, r)).start()

    for j in range(CHUNKS):
        loads(j).wait()
        for q in range(width // rows):
            block = stage[j, :, q * rows : (q + 1) * rows].T
            high = block.astype(jnp.bfloat16)
            at_row = j * width + q * rows
            at[at_row : at_row + rows, 0:rows] = high
            at[at_row : at_row + rows, rows : 2 * rows] = (block - high.astype(jnp.float32)).astype(
                jnp.bfloat16
            )

    @pl.when(t == 1)
    def _():
        copy(ls, lb.at[r], LBR, (t, r)).wait_recv()
        spread(lb.at[r], lb.at[r], LB)

    arrived(g0, G0)
    for p in range(parts):
        fill(0, p, g0[p, 0:members])
        fill(1, p, g0[p, members : 2 * members])
    image_f, image_c = product(2)
    own_f, own_c = f_ref[...], c_ref[...]
    image_f = image_f - damp * own_f
    image_c = image_c - damp * own_c
    forcing = lambda p: g0[p, 0:members]
    initial = lambda p: g0[p, members : 2 * members]

    @pl.when(t == 0)
    def _():
        prs[0:members] = image_f
        prs[members : 2 * members] = image_c
        copy(prs, pr.at[r], PRR, (t + 1, r)).start()
        gu[r] = image_c
        spread(gu.at[r], gu.at[r], GU)
        gf[r] = image_f
        spread(gf.at[r], gf.at[r], GF)
        arrived(gu, GU)
        known_c, (t0c, t1c) = second_step(initial, lambda p: gu[p], own_c, image_c)
        arrived(gf, GF)
        known_f, (t0f, t1f) = second_step(forcing, lambda p: gf[p], own_f, image_f)
        tb[r] = packed([t0c, t1c, t0f, t1f, h])
        spread_next(tb.at[r], tp.at[r], TP)
        spread(tb.at[r], tb.at[r], TB)
        arrived(tb, TB)
        t0c, t1c, t0f, t1f = unpacked(tb, 4)
        x1, x2 = start_weights(h, known_c, t0c, t1c)
        x3, x4 = forcing_weights(h, known_f, t0f, t1f)
        o_ref[...] = x1 * own_c + x2 * image_c + (x3 * own_f + x4 * image_f)

    @pl.when(t > 0)
    def _():
        gf[r] = image_f
        spread(gf.at[r], gf.at[r], GF)

        def pass_on():
            copy(prs, pr.at[r], PRR, (t, r)).wait_recv()
            spread(pr.at[r], pr.at[r], PR)

        pl.when(t == 1)(pass_on)
        arrived(gf, GF)
        known_f, (t0f, t1f) = second_step(forcing, lambda p: gf[p], own_f, image_f)
        tf[r] = packed([t0f, t1f])
        spread(tf.at[r], tf.at[r], TF)
        arrived(tf, TF)
        x3, x4 = forcing_weights(h, known_f, *unpacked(tf, 2))
        local = x3 * own_f + x4 * image_f

        @pl.when(t + 1 < slabs)
        def _():
            ls[...] = local
            copy(ls, lb.at[r], LBR, (t + 1, r)).start()

        @pl.when(t > 1)
        def _():
            copy(ls, lb.at[r], LBR, (t, r)).wait_recv()
            spread(lb.at[r], lb.at[r], LB)

        pl.when(t > 1)(pass_on)
        arrived(lb, LB)
        for p in range(parts):
            fill(0, p, lb[p])
        image_l = product(1)[0] - damp * lb[r]
        arrived(pr, PR)
        for p in range(parts):
            fill(0, p, pr[p, 0:members])
            fill(1, p, pr[p, members : 2 * members])
        image_p, image_u = product(2)
        last_p, last_u = pr[r, 0:members], pr[r, members : 2 * members]
        image_p = image_p - damp * last_p
        image_u = image_u - damp * last_u

        early = t == 1
        last_c = lambda p: jnp.where(early, g0[p, members : 2 * members], pr[p, 0:members])
        last_w = lambda p: pr[p, members : 2 * members]
        b2, g = moments(last_c, last_w)
        known_c = (b2, g, jnp.sqrt(remainder(last_c, last_w, g, False) / b2 + EPSILON))
        last_f, last_v = (lambda p: lb[p]), (lambda p: pr[p, 0:members])
        b2, g = moments(last_f, last_v)
        known_l = (b2, g, jnp.sqrt(remainder(last_f, last_v, g, False) / b2 + EPSILON))
        arrived(tp, TP, parts)
        t0c, t1c, t0l, t1l, hs = unpacked(tp, 5)
        hs = hs * (1.0 / parts)
        x1, x2 = start_weights(hs, known_c, t0c, t1c)
        x3, x4 = forcing_weights(hs, known_l, t0l, t1l)
        one = jnp.ones_like(x1)
        e1 = jnp.where(early, x1, 0.0 * one)
        e2 = jnp.where(early, x4, x1)
        e4 = jnp.where(early, x3, one)
        own = e1 * own_c + e2 * last_p + x2 * last_u + e4 * lb[r]
        image = e1 * image_c + e2 * image_p + x2 * image_u + e4 * image_l

        @pl.when(t + 1 < slabs)
        def _():
            prs[0:members] = own
            prs[members : 2 * members] = image
            copy(prs, pr.at[r], PRR, (t + 1, r)).start()

        gu[r] = image
        spread(gu.at[r], gu.at[r], GU)
        for p in range(parts):
            ck[p] = (
                e1 * g0[p, members : 2 * members]
                + e2 * pr[p, 0:members]
                + x2 * pr[p, members : 2 * members]
                + e4 * lb[p]
            )
        arrived(gu, GU)
        known, (t0, t1) = second_step(lambda p: ck[p], lambda p: gu[p], own, image)
        tb[r] = packed([t0, t1, None, None, h])

        @pl.when(t + 1 < slabs)
        def _():
            spread_next(tb.at[r], tp.at[r], TP)

        spread(tb.at[r], tb.at[r], TB)
        arrived(tb, TB)
        x1, x2 = start_weights(h, known, *unpacked(tb, 2))
        o_ref[...] = x1 * own + x2 * image + local

    left(g0, G0)
    left(gf, GF)
    left(gu, GU)
    left(tb, TB)

    @pl.when(t + 1 < slabs)
    def _():
        copy(ls, lb.at[r], LBR, (t, r)).wait_send()
        copy(prs, pr.at[r], PRR, (t, r)).wait_send()
        left(tp, TP, parts)

    @pl.when(t > 0)
    def _():
        left(lb, LB)
        left(pr, PR)
        left(tf, TF)


def on_device(parts, slabs, coupling, damping, forcing, initial, counts):
    members, rows = initial.shape
    whole = coupling.shape[2]
    vmem, ram = pl.BlockSpec(memory_space=pltpu.VMEM), pl.BlockSpec(memory_space=pltpu.SMEM)
    blocks = lambda height: pltpu.VMEM((parts, height, rows), jnp.float32)
    scalars = pltpu.VMEM((parts, 1, LANES), jnp.float32)
    result = pl.pallas_call(
        functools.partial(kernel, members, rows, parts, slabs),
        out_shape=jax.ShapeDtypeStruct((members, rows), jnp.float32),
        in_specs=[pl.BlockSpec(memory_space=pl.ANY), vmem, vmem, vmem, ram],
        out_specs=vmem,
        scratch_shapes=[
            pltpu.VMEM((CHUNKS, rows, whole // CHUNKS), jnp.float32),
            pltpu.VMEM((whole, 2 * rows), jnp.bfloat16),
            pltpu.VMEM((4 * members, whole), jnp.bfloat16),
            blocks(2 * members), blocks(members), blocks(members), blocks(members),
            blocks(2 * members), blocks(members), scalars, scalars, scalars,
            pltpu.VMEM((members, rows), jnp.float32),
            pltpu.VMEM((2 * members, rows), jnp.float32),
            pltpu.SemaphoreType.DMA((CHUNKS,)),
            pltpu.SemaphoreType.DMA((10,)),
            pltpu.SemaphoreType.DMA((10,)),
        ],
        compiler_params=pltpu.CompilerParams(
            collective_id=0, has_side_effects=True, vmem_limit_bytes=40 << 20
        ),
    )(coupling, damping, forcing[0], initial, counts)
    return result[None]


def solution(mesh):
    placed = (P("tm", "row", None), P("tm", "row"), P("tm", None, "row"), P(None, "row"), P("tm"))
    step = functools.partial(on_device, mesh.shape["row"], mesh.shape["tm"])
    return jax.shard_map(
        step, mesh=mesh, in_specs=placed, out_specs=P("tm", None, "row"), check_vma=False
    )
```

```python
import functools

import jax
import jax.numpy as jnp
from jax import lax
from jax.experimental import pallas as pl
from jax.experimental.pallas import tpu as pltpu
from jax.sharding import PartitionSpec as P

MESH = pl.DeviceIdType.MESH
TIME_STEP = 0.125
EPSILON = 1e-06
SQUARINGS = 5
TAYLOR_TERMS = 12
SIDE = 4
LANES = 128
CHUNKS = 8


def steps():
    hops = lambda d: min(d, SIDE - d)
    chips = [(z, y) for z in range(SIDE) for y in range(SIDE)]
    chips.sort(key=lambda s: (-hops(s[0]) - hops(s[1]), -abs(hops(s[0]) - hops(s[1]))))
    found = [(hops(z) + hops(y), z, y, flip) for z, y in chips for flip in (0, 1)]
    return found[:-2] + [found[-1], found[-2]]


STEPS = steps()
GROUPS = ((0, 10), (10, 22), (22, 32))


def exponential(h, g, below, above, corner):
    scale = h * (1.0 / 2.0**SQUARINGS)
    s00, s01, s10, s11 = g * scale, above * scale, below * scale, corner * scale
    edge = 1.0 / 2.0**SQUARINGS
    one, zero = jnp.ones_like(s00), jnp.zeros_like(s00)
    r00, r01, r10, r11, c0, c1 = one, zero, zero, one, zero, zero
    for degree in range(TAYLOR_TERMS, 0, -1):
        f = 1.0 / degree
        r00, r01, r10, r11, c0, c1 = (
            1.0 + (s00 * r00 + s01 * r10) * f,
            (s00 * r01 + s01 * r11) * f,
            (s10 * r00 + s11 * r10) * f,
            1.0 + (s10 * r01 + s11 * r11) * f,
            (s00 * c0 + s01 * c1 + edge) * f,
            (s10 * c0 + s11 * c1) * f,
        )
    for _ in range(SQUARINGS):
        r00, r01, r10, r11, c0, c1 = (
            r00 * r00 + r01 * r10,
            r00 * r01 + r01 * r11,
            r10 * r00 + r11 * r10,
            r10 * r01 + r11 * r11,
            r00 * c0 + r01 * c1 + c0,
            r10 * c0 + r11 * c1 + c1,
        )
    return r00, r10, c0, c1


def kernel(
    members, rows, parts, slabs,
    a_hbm, damp_hbm, f_hbm, c_hbm, n_ref, o_ref,
    stage, at, xs, cb, fb, lb, pu, pa, gf, gu, ck, tb, tf, tp, ls, damp_ref,
    a_sem, small_sem, ready, send, recv, recv_one,
):
    t, r = lax.axis_index("tm"), lax.axis_index("row")
    core, chip = lax.rem(r, 2), r // 2
    z, y = chip // SIDE, lax.rem(chip, SIDE)
    zs = [lax.rem(z + d, SIDE) * (2 * SIDE) for d in range(SIDE)]
    ys = [lax.rem(y + d, SIDE) * 2 for d in range(SIDE)]
    cores = (core, 1 - core)
    width = a_hbm.shape[2] // CHUNKS
    C, F, LB, PU, PA, GF, GU, LBR, PUR, PAR, TF, TB, TP = range(13)
    last = parts - 1

    def loads(j):
        return pltpu.make_async_copy(
            a_hbm.at[0, :, pl.ds(j * width, width)], stage.at[:, pl.ds(j * width, width)], a_sem.at[j]
        )

    small = [
        pltpu.make_async_copy(from_ref, to_ref, small_sem.at[i])
        for i, (from_ref, to_ref) in enumerate(
            ((f_hbm, fb.at[last]), (c_hbm, cb.at[last]), (damp_hbm, damp_ref))
        )
    ]

    def copy(src, dst, k, arrival, device):
        return pltpu.make_async_remote_copy(
            src_ref=src, dst_ref=dst, send_sem=send.at[k], recv_sem=arrival,
            device_id=device, device_id_type=MESH,
        )

    def relay(src, dst, k):
        return copy(src, dst.at[last], k, recv_one.at[k], (t + 1, r))

    def spread(buffer, k):
        for group, (low, high) in enumerate(GROUPS):
            for i in range(low, min(high, last)):
                _, dz, dy, flip = STEPS[i]
                copy(
                    buffer.at[last], buffer.at[i], k, recv.at[k, group], (t, zs[dz] + ys[dy] + cores[flip])
                ).start()

    def spread_sums(buffer, k):
        for i in range(last):
            _, dz, dy, flip = STEPS[i]
            copy(
                buffer.at[last], buffer.at[i], k, recv_one.at[k], (t, zs[dz] + ys[dy] + cores[flip])
            ).start()

    def spread_next():
        for _, dz, dy, flip in STEPS:
            i = STEPS.index((_, dz, dy, flip))
            copy(
                tb.at[last], tp.at[i], TP, recv_one.at[TP], (t + 1, zs[dz] + ys[dy] + cores[flip])
            ).start()

    def arrived(buffer, k, group):
        low, high = GROUPS[group]
        some = buffer.at[pl.ds(0, min(high, last) - low)]
        pltpu.make_async_copy(some, some, recv.at[k, group]).wait()

    def took(buffer, semaphore, count):
        some = buffer.at[pl.ds(0, count)]
        pltpu.make_async_copy(some, some, semaphore).wait()

    def fill(at_part, v):
        high = v.astype(jnp.bfloat16).astype(jnp.float32)
        both = jnp.concatenate([high, v - high], axis=0).astype(jnp.bfloat16)
        xs[:, rows * at_part : rows * at_part + rows] = both

    def applied(buffer, k, beside=None):
        total = jnp.zeros((2 * members, 2 * rows), jnp.float32)
        n2 = jnp.zeros((members, rows), jnp.float32)
        d = jnp.zeros((members, rows), jnp.float32)
        if beside is not None:
            for p in range(parts):
                n2 += beside[p] * beside[p]
            b2 = jnp.sum(n2, axis=1, keepdims=True) + EPSILON
        for group, (low, high) in enumerate(GROUPS):
            arrived(buffer, k, group)
            for p in range(low, high):
                v = buffer[p]
                fill(p, v)
                if beside is not None:
                    d += beside[p] * v
            total += jnp.dot(
                xs[:, rows * low : rows * high], at[rows * low : rows * high, :],
                preferred_element_type=jnp.float32,
            )
        top, under = total[:members], total[members:]
        image = top[:, :rows] + (top[:, rows:] + under[:, :rows]) - damp * buffer[last]
        if beside is None:
            return image
        return image, b2, jnp.sum(d, axis=1, keepdims=True) / b2

    def below(first, second, b2, g):
        w2 = jnp.zeros((members, rows), jnp.float32)
        for p in range(parts):
            w = second[p] - g * first[p]
            w2 += w * w
        return jnp.sqrt(jnp.sum(w2, axis=1, keepdims=True) / b2 + EPSILON)

    def sums(first, second, image, g):
        w = second - g * first
        image = image - g * second
        return (
            jnp.sum(first * image, axis=1, keepdims=True),
            jnp.sum(w * image, axis=1, keepdims=True),
        )

    lane = lax.broadcasted_iota(jnp.int32, (members, LANES), 1)
    member = lax.broadcasted_iota(jnp.int32, (members, LANES), 0)

    def packed(columns):
        row = jnp.zeros((members, LANES), jnp.float32)
        for j, column in enumerate(columns):
            if column is not None:
                row = jnp.where(lane == member + members * j, column, row)
        return jnp.sum(row, axis=0, keepdims=True)

    def unpacked(buffer, count):
        total = jnp.sum(buffer[...], axis=0)
        total = jnp.broadcast_to(total, (members, LANES))
        return [
            jnp.sum(jnp.where(lane == member + members * j, total, 0.0), axis=1, keepdims=True)
            for j in range(count)
        ]

    def start_weights(h, known, t0, t1):
        b2, g, side = known
        e00, e10, _, _ = exponential(h, g, side, t0 / (b2 * side), t1 / (b2 * side * side))
        x2 = e10 / side
        return e00 - g * x2, x2

    def forcing_weights(h, known, t0, t1):
        b2, g, side = known
        _, _, c0, c1 = exponential(h, g, side, t0 / (b2 * side), t1 / (b2 * side * side))
        x4 = h * c1 / side
        return h * c0 - g * x4, x4

    for copy_in in small:
        copy_in.start()
    for j in range(CHUNKS):
        loads(j).start()

    barrier = pltpu.get_barrier_semaphore()
    for _, dz, dy, flip in STEPS[:-1]:
        pl.semaphore_signal(
            barrier, inc=1, device_id=(t, zs[dz] + ys[dy] + cores[flip]), device_id_type=MESH
        )

    @pl.when(t > 0)
    def _():
        pl.semaphore_signal(barrier, inc=1, device_id=(t - 1, r), device_id_type=MESH)

    @pl.when(t + 1 < slabs)
    def _():
        pl.semaphore_signal(barrier, inc=1, device_id=(t + 1, r), device_id_type=MESH)

    for copy_in in small:
        copy_in.wait()
    h = jnp.full((members, 1), n_ref[0].astype(jnp.float32) * TIME_STEP, jnp.float32)
    damp = damp_ref[...]
    pl.semaphore_wait(barrier, last + jnp.minimum(t, 1) + jnp.minimum(slabs - 1 - t, 1))

    @pl.when(t > 0)
    def _():
        pl.semaphore_signal(ready, inc=1, device_id=(t - 1, r), device_id_type=MESH)

    @pl.when(t == 0)
    def _():
        relay(fb.at[last], lb, LBR).start()
        spread(cb, C)

    spread(fb, F)

    @pl.when(t == 1)
    def _():
        spread(cb, C)

    for j in range(CHUNKS):
        loads(j).wait()
    for i, (_, dz, dy, flip) in enumerate(STEPS):
        source = zs[(SIDE - dz) % SIDE] + ys[(SIDE - dy) % SIDE] + cores[flip]
        block = stage[:, pl.ds(pl.multiple_of(source * rows, rows), rows)].T
        high = block.astype(jnp.bfloat16)
        at[i * rows : (i + 1) * rows, 0:rows] = high
        at[i * rows : (i + 1) * rows, rows : 2 * rows] = (block - high.astype(jnp.float32)).astype(
            jnp.bfloat16
        )

    own_f = fb[last]

    @pl.when(t == 0)
    def _():
        own_c = cb[last]
        image_c = applied(cb, C)
        gu[last] = image_c
        relay(gu.at[last], pu, PUR).start()
        spread(gu, GU)
        image_f = applied(fb, F)
        gf[last] = image_f
        relay(gf.at[last], pa, PAR).start()
        spread(gf, GF)
        image, b2, g = applied(gu, GU, cb)
        t0c, t1c = sums(own_c, image_c, image, g)
        known_c = (b2, g, below(cb, gu, b2, g))
        image, b2, g = applied(gf, GF, fb)
        t0f, t1f = sums(own_f, image_f, image, g)
        tb[last] = packed([t0c, t1c, t0f, t1f, h])
        pl.semaphore_wait(ready, 1)
        spread_next()
        spread_sums(tb, TB)
        known_f = (b2, g, below(fb, gf, b2, g))
        took(tb, recv_one.at[TB], last)
        t0c, t1c, t0f, t1f = unpacked(tb, 4)
        x1, x2 = start_weights(h, known_c, t0c, t1c)
        x3, x4 = forcing_weights(h, known_f, t0f, t1f)
        o_ref[...] = x1 * own_c + x2 * image_c + (x3 * own_f + x4 * image_f)

    def later(early):
        def pass_on(buffer, one, k):
            copy(ls, buffer.at[last], k, recv_one.at[one], (t, r)).wait_recv()
            spread(buffer, k)

        if early:
            pass_on(lb, LBR, LB)
        image_f = applied(fb, F)
        gf[last] = image_f
        spread(gf, GF)
        if early:
            image_c = applied(cb, C)
            pass_on(pu, PUR, PU)
            pass_on(pa, PAR, PA)
            image_l = applied(lb, LB)
        image, b2, g = applied(gf, GF, fb)
        tf[last] = packed(list(sums(own_f, image_f, image, g)))
        spread_sums(tf, TF)
        known_f = (b2, g, below(fb, gf, b2, g))

        def finish_forcing():
            took(tf, recv_one.at[TF], last)
            x3, x4 = forcing_weights(h, known_f, *unpacked(tf, 2))
            local = x3 * own_f + x4 * image_f

            @pl.when(t + 1 < slabs)
            def _():
                ls[...] = local
                copy(ls, lb.at[last], LBR, recv_one.at[LBR], (t + 1, r)).start()

            return local

        if early:
            image_u, b2c, gc = applied(pu, PU, cb)
            known_c = (b2c, gc, below(cb, pu, b2c, gc))
            image_p, b2l, gl = applied(pa, PA, lb)
            known_l = (b2l, gl, below(lb, pa, b2l, gl))
            local = finish_forcing()
        else:
            local = finish_forcing()
            pass_on(lb, LBR, LB)
            pass_on(pu, PUR, PU)
            pass_on(pa, PAR, PA)
            image_l = applied(lb, LB)
            image_u = applied(pu, PU)
            image_p, b2c, gc = applied(pa, PA, pu)
            n2 = jnp.zeros((members, rows), jnp.float32)
            for p in range(parts):
                n2 += pa[p] * pa[p]
            b2u = b2c
            b2c = jnp.sum(n2, axis=1, keepdims=True) + EPSILON
            gc = gc * b2u / b2c
            known_c = (b2c, gc, below(pa, pu, b2c, gc))
        took(tp, recv_one.at[TP], parts)
        t0c, t1c, t0l, t1l, hs = unpacked(tp, 5)
        hs = hs * (1.0 / parts)
        x1, x2 = start_weights(hs, known_c, t0c, t1c)
        if early:
            x3, x4 = forcing_weights(hs, known_l, t0l, t1l)
            state = lambda p: x1 * cb[p] + x2 * pu[p] + (x3 * lb[p] + x4 * pa[p])
            image = x1 * image_c + x2 * image_u + (x3 * image_l + x4 * image_p)
        else:
            state = lambda p: x1 * pa[p] + x2 * pu[p] + lb[p]
            image = x1 * image_p + x2 * image_u + image_l
        gu[last] = image
        ck[last] = state(last)

        @pl.when(t + 1 < slabs)
        def _():
            relay(gu.at[last], pu, PUR).start()
            relay(ck.at[last], pa, PAR).start()

        spread(gu, GU)
        for p in range(last):
            ck[p] = state(p)
        own = ck[last]
        again, b2, g = applied(gu, GU, ck)
        tb[last] = packed([*sums(own, image, again, g), None, None, h])

        @pl.when(t + 1 < slabs)
        def _():
            pl.semaphore_wait(ready, 1)
            spread_next()

        spread_sums(tb, TB)
        known = (b2, g, below(ck, gu, b2, g))
        took(tb, recv_one.at[TB], last)
        x1, x2 = start_weights(h, known, *unpacked(tb, 2))
        o_ref[...] = x1 * own + x2 * image + local

    pl.when(t == 1)(functools.partial(later, True))
    pl.when(t > 1)(functools.partial(later, False))

    for buffer, k in ((fb, F), (gf, GF), (gu, GU), (tb, TB)):
        took(buffer, send.at[k], last)

    @pl.when(t < 2)
    def _():
        took(cb, send.at[C], last)

    @pl.when(t + 1 < slabs)
    def _():
        for k in (LBR, PUR, PAR):
            took(lb, send.at[k], 1)
        took(tp, send.at[TP], parts)

    @pl.when(t > 0)
    def _():
        for buffer, k in ((lb, LB), (pu, PU), (pa, PA), (tf, TF)):
            took(buffer, send.at[k], last)


def on_device(parts, slabs, coupling, damping, forcing, initial, counts):
    members, rows = initial.shape
    whole = coupling.shape[2]
    far, ram = pl.BlockSpec(memory_space=pl.ANY), pl.BlockSpec(memory_space=pltpu.SMEM)
    blocks = pltpu.VMEM((parts, members, rows), jnp.float32)
    scalars = pltpu.VMEM((parts, 1, LANES), jnp.float32)
    result = pl.pallas_call(
        functools.partial(kernel, members, rows, parts, slabs),
        out_shape=jax.ShapeDtypeStruct((members, rows), jnp.float32),
        in_specs=[far, far, far, far, ram],
        out_specs=pl.BlockSpec(memory_space=pltpu.VMEM),
        scratch_shapes=[
            pltpu.VMEM((rows, whole), jnp.float32),
            pltpu.VMEM((whole, 2 * rows), jnp.bfloat16),
            pltpu.VMEM((2 * members, whole), jnp.bfloat16),
            *[blocks] * 8,
            *[scalars] * 3,
            pltpu.VMEM((members, rows), jnp.float32),
            pltpu.VMEM((1, rows), jnp.float32),
            pltpu.SemaphoreType.DMA((CHUNKS,)),
            pltpu.SemaphoreType.DMA((3,)),
            pltpu.SemaphoreType.REGULAR,
            pltpu.SemaphoreType.DMA((13,)),
            pltpu.SemaphoreType.DMA((7, len(GROUPS))),
            pltpu.SemaphoreType.DMA((13,)),
        ],
        compiler_params=pltpu.CompilerParams(
            collective_id=0, has_side_effects=True, vmem_limit_bytes=60 << 20
        ),
    )(coupling, damping, forcing[0], initial, counts)
    return result[None]


def solution(mesh):
    placed = (P("tm", "row", None), P("tm", "row"), P("tm", None, "row"), P(None, "row"), P("tm"))
    step = functools.partial(on_device, mesh.shape["row"], mesh.shape["tm"])
    return jax.shard_map(
        step, mesh=mesh, in_specs=placed, out_specs=P("tm", None, "row"), check_vma=False
    )
```

```python
import functools

import jax
import jax.numpy as jnp
from jax import lax
from jax.experimental import pallas as pl
from jax.experimental.pallas import tpu as pltpu
from jax.sharding import PartitionSpec as P

MESH = pl.DeviceIdType.MESH
TIME_STEP = 0.125
EPSILON = 1e-06
SQUARINGS = 5
TAYLOR_TERMS = 12
SIDE = 4
LANES = 128
CHUNKS = 8


def steps():
    hops = lambda d: min(d, SIDE - d)
    chips = [(z, y) for z in range(SIDE) for y in range(SIDE)]
    chips.sort(key=lambda s: (-hops(s[0]) - hops(s[1]), -abs(hops(s[0]) - hops(s[1]))))
    return [(z, y, flip) for flip in (0, 1) for z, y in chips]


STEPS = steps()
CHIPS = len(STEPS) // 2
OWN = CHIPS - 1
GROUPS = ((0, 5), (5, 11), (11, 15))
BY_DISTANCE = [i + CHIPS * flip for i in range(CHIPS) for flip in (0, 1)]


def exponential(h, g, below, above, corner):
    scale = h * (1.0 / 2.0**SQUARINGS)
    s00, s01, s10, s11 = g * scale, above * scale, below * scale, corner * scale
    edge = 1.0 / 2.0**SQUARINGS
    one, zero = jnp.ones_like(s00), jnp.zeros_like(s00)
    r00, r01, r10, r11, c0, c1 = one, zero, zero, one, zero, zero
    for degree in range(TAYLOR_TERMS, 0, -1):
        f = 1.0 / degree
        r00, r01, r10, r11, c0, c1 = (
            1.0 + (s00 * r00 + s01 * r10) * f,
            (s00 * r01 + s01 * r11) * f,
            (s10 * r00 + s11 * r10) * f,
            1.0 + (s10 * r01 + s11 * r11) * f,
            (s00 * c0 + s01 * c1 + edge) * f,
            (s10 * c0 + s11 * c1) * f,
        )
    for _ in range(SQUARINGS):
        r00, r01, r10, r11, c0, c1 = (
            r00 * r00 + r01 * r10,
            r00 * r01 + r01 * r11,
            r10 * r00 + r11 * r10,
            r10 * r01 + r11 * r11,
            r00 * c0 + r01 * c1 + c0,
            r10 * c0 + r11 * c1 + c1,
        )
    return r00, r10, c0, c1


def kernel(
    members, rows, parts, slabs,
    a_hbm, damp_hbm, f_hbm, c_hbm, n_ref, o_ref,
    stage, at, xs, cb, fb, lb, pu, pa, gf, gu, ck, tb, tf, tp, ls, damp_ref,
    a_sem, small_sem, ready, send, recv, recv_one,
):
    t, r = lax.axis_index("tm"), lax.axis_index("row")
    core, chip = lax.rem(r, 2), r // 2
    z, y = chip // SIDE, lax.rem(chip, SIDE)
    zs = [lax.rem(z + d, SIDE) * (2 * SIDE) for d in range(SIDE)]
    ys = [lax.rem(y + d, SIDE) * 2 for d in range(SIDE)]
    cores = (core, 1 - core)
    width = a_hbm.shape[2] // CHUNKS
    C, F, LB, PU, PA, GF, GU, LBR, PUR, PAR, TF, TB, TP = range(13)
    last = parts - 1

    def loads(j):
        return pltpu.make_async_copy(
            a_hbm.at[0, :, pl.ds(j * width, width)], stage.at[:, pl.ds(j * width, width)], a_sem.at[j]
        )

    small = [
        pltpu.make_async_copy(from_ref, to_ref, small_sem.at[i])
        for i, (from_ref, to_ref) in enumerate(
            ((f_hbm, fb.at[OWN]), (c_hbm, cb.at[OWN]), (damp_hbm, damp_ref))
        )
    ]

    def copy(src, dst, k, arrival, device):
        return pltpu.make_async_remote_copy(
            src_ref=src, dst_ref=dst, send_sem=send.at[k], recv_sem=arrival,
            device_id=device, device_id_type=MESH,
        )

    def device(i):
        dz, dy, flip = STEPS[i]
        return zs[dz] + ys[dy] + cores[flip]

    def relay(src, dst, k):
        return copy(src, dst.at[OWN], k, recv_one.at[k], (t + 1, r))

    def spread(buffer, k):
        own = buffer.at[OWN]
        for group, (low, high) in enumerate(GROUPS):
            for i in range(low, high):
                copy(own, buffer.at[i], k, recv.at[k, group], (t, device(i))).start()
        copy(own, buffer.at[last], k, recv.at[k, 2 * len(GROUPS) - 1], (t, device(last))).start()

    def forward(buffer, k):
        for group, (low, high) in enumerate(GROUPS):
            took(buffer, recv.at[k, group], high - low)
            copy(
                buffer.at[pl.ds(low, high - low)], buffer.at[pl.ds(CHIPS + low, high - low)],
                k, recv.at[k, len(GROUPS) + group], (t, device(last)),
            ).start()

    def spread_sums(buffer, k):
        for i in BY_DISTANCE:
            if i != OWN:
                copy(buffer.at[OWN], buffer.at[i], k, recv_one.at[k], (t, device(i))).start()

    def spread_next():
        for i in BY_DISTANCE:
            copy(tb.at[OWN], tp.at[i], TP, recv_one.at[TP], (t + 1, device(i))).start()

    def took(buffer, semaphore, count):
        some = buffer.at[pl.ds(0, count)]
        pltpu.make_async_copy(some, some, semaphore).wait()

    def fill(slot, at_part, v):
        high = v.astype(jnp.bfloat16).astype(jnp.float32)
        both = jnp.concatenate([high, v - high], axis=0).astype(jnp.bfloat16)
        xs[16 * slot : 16 * slot + 16, rows * at_part : rows * at_part + rows] = both

    def applied(*gathers):
        count = len(gathers)
        total = jnp.zeros((2 * members * count, 2 * rows), jnp.float32)
        norms, d = {}, {}
        for j, (buffer, k, *beside) in enumerate(gathers):
            forward(buffer, k)
            if beside:
                n2 = jnp.zeros((members, rows), jnp.float32)
                d[j] = jnp.zeros((members, rows), jnp.float32)
                if not any(beside[0] is earlier[0] for earlier in gathers):
                    for p in range(parts):
                        n2 += beside[0][p] * beside[0][p]
                norms[j] = n2
        ends = [0, CHIPS, *(CHIPS + high for _, high in GROUPS[:-1]), parts]
        for group, (low, high) in enumerate(zip(ends, ends[1:])):
            for j, (buffer, k, *_) in enumerate(gathers):
                if group > 0:
                    took(buffer, recv.at[k, len(GROUPS) + group - 1], high - low)
                for p in range(low, high):
                    fill(j, p, buffer[p])
            for j, (buffer, _, *beside) in enumerate(gathers):
                if beside:
                    for p in range(low, high):
                        d[j] += beside[0][p] * buffer[p]
                        if any(beside[0] is earlier[0] for earlier in gathers):
                            norms[j] += beside[0][p] * beside[0][p]
            total += jnp.dot(
                xs[0 : 16 * count, rows * low : rows * high], at[rows * low : rows * high, :],
                preferred_element_type=jnp.float32,
            )
        out = []
        for j, (buffer, _, *beside) in enumerate(gathers):
            at_row = 2 * members * j
            top, under = total[at_row : at_row + members], total[at_row + members : at_row + 2 * members]
            image = top[:, :rows] + (top[:, rows:] + under[:, :rows]) - damp * buffer[OWN]
            if beside:
                b2 = jnp.sum(norms[j], axis=1, keepdims=True) + EPSILON
                out.append((image, b2, jnp.sum(d[j], axis=1, keepdims=True) / b2))
            else:
                out.append(image)
        return out[0] if count == 1 else out

    def below(first, second, b2, g):
        w2 = jnp.zeros((members, rows), jnp.float32)
        for p in range(parts):
            w = second[p] - g * first[p]
            w2 += w * w
        return jnp.sqrt(jnp.sum(w2, axis=1, keepdims=True) / b2 + EPSILON)

    def sums(first, second, image, g):
        w = second - g * first
        image = image - g * second
        return (
            jnp.sum(first * image, axis=1, keepdims=True),
            jnp.sum(w * image, axis=1, keepdims=True),
        )

    lane = lax.broadcasted_iota(jnp.int32, (members, LANES), 1)
    member = lax.broadcasted_iota(jnp.int32, (members, LANES), 0)

    def packed(columns):
        row = jnp.zeros((members, LANES), jnp.float32)
        for j, column in enumerate(columns):
            if column is not None:
                row = jnp.where(lane == member + members * j, column, row)
        return jnp.sum(row, axis=0, keepdims=True)

    def unpacked(buffer, count):
        total = jnp.sum(buffer[...], axis=0)
        total = jnp.broadcast_to(total, (members, LANES))
        return [
            jnp.sum(jnp.where(lane == member + members * j, total, 0.0), axis=1, keepdims=True)
            for j in range(count)
        ]

    def start_weights(h, known, t0, t1):
        b2, g, side = known
        e00, e10, _, _ = exponential(h, g, side, t0 / (b2 * side), t1 / (b2 * side * side))
        x2 = e10 / side
        return e00 - g * x2, x2

    def forcing_weights(h, known, t0, t1):
        b2, g, side = known
        _, _, c0, c1 = exponential(h, g, side, t0 / (b2 * side), t1 / (b2 * side * side))
        x4 = h * c1 / side
        return h * c0 - g * x4, x4

    for copy_in in small:
        copy_in.start()
    for j in range(CHUNKS):
        loads(j).start()

    barrier = pltpu.get_barrier_semaphore()
    for i in (*range(OWN), last):
        pl.semaphore_signal(barrier, inc=1, device_id=(t, device(i)), device_id_type=MESH)

    @pl.when(t > 0)
    def _():
        pl.semaphore_signal(barrier, inc=1, device_id=(t - 1, r), device_id_type=MESH)

    @pl.when(t + 1 < slabs)
    def _():
        pl.semaphore_signal(barrier, inc=1, device_id=(t + 1, r), device_id_type=MESH)

    for copy_in in small:
        copy_in.wait()
    h = jnp.full((members, 1), n_ref[0].astype(jnp.float32) * TIME_STEP, jnp.float32)
    damp = damp_ref[...]
    pl.semaphore_wait(barrier, CHIPS + jnp.minimum(t, 1) + jnp.minimum(slabs - 1 - t, 1))

    @pl.when(t == 0)
    def _():
        relay(fb.at[OWN], lb, LBR).start()
        spread(cb, C)

    spread(fb, F)

    @pl.when(t == 1)
    def _():
        spread(cb, C)

    for j in range(CHUNKS):
        loads(j).wait()
    for i, (dz, dy, flip) in enumerate(STEPS):
        source = zs[(SIDE - dz) % SIDE] + ys[(SIDE - dy) % SIDE] + cores[flip]
        block = stage[:, pl.ds(pl.multiple_of(source * rows, rows), rows)].T
        high = block.astype(jnp.bfloat16)
        at[i * rows : (i + 1) * rows, 0:rows] = high
        at[i * rows : (i + 1) * rows, rows : 2 * rows] = (block - high.astype(jnp.float32)).astype(
            jnp.bfloat16
        )

    own_f = fb[OWN]

    @pl.when(t == 0)
    def _():
        own_c = cb[OWN]
        image_c = applied((cb, C))
        gu[OWN] = image_c
        relay(gu.at[OWN], pu, PUR).start()
        spread(gu, GU)
        image_f = applied((fb, F))
        gf[OWN] = image_f
        relay(gf.at[OWN], pa, PAR).start()
        spread(gf, GF)
        image, b2, g = applied((gu, GU, cb))
        t0c, t1c = sums(own_c, image_c, image, g)
        known_c = (b2, g, below(cb, gu, b2, g))
        image, b2, g = applied((gf, GF, fb))
        t0f, t1f = sums(own_f, image_f, image, g)
        tb[OWN] = packed([t0c, t1c, t0f, t1f, h])
        pl.semaphore_wait(ready, 1)
        spread_next()
        spread_sums(tb, TB)
        known_f = (b2, g, below(fb, gf, b2, g))
        took(tb, recv_one.at[TB], last)
        t0c, t1c, t0f, t1f = unpacked(tb, 4)
        x1, x2 = start_weights(h, known_c, t0c, t1c)
        x3, x4 = forcing_weights(h, known_f, t0f, t1f)
        o_ref[...] = x1 * own_c + x2 * image_c + (x3 * own_f + x4 * image_f)

    def later(early):
        def pass_on(buffer, one, k):
            copy(ls, buffer.at[OWN], k, recv_one.at[one], (t, r)).wait_recv()
            spread(buffer, k)

        if early:
            pass_on(lb, LBR, LB)
        image_f = applied((fb, F))
        pl.semaphore_signal(ready, inc=1, device_id=(t - 1, r), device_id_type=MESH)
        gf[OWN] = image_f
        spread(gf, GF)
        if early:
            image_c = applied((cb, C))
            pass_on(pu, PUR, PU)
            pass_on(pa, PAR, PA)
        image, b2, g = applied((gf, GF, fb))
        tf[OWN] = packed(list(sums(own_f, image_f, image, g)))
        spread_sums(tf, TF)
        known_f = (b2, g, below(fb, gf, b2, g))

        def finish_forcing():
            took(tf, recv_one.at[TF], last)
            x3, x4 = forcing_weights(h, known_f, *unpacked(tf, 2))
            local = x3 * own_f + x4 * image_f

            @pl.when(t + 1 < slabs)
            def _():
                ls[...] = local
                copy(ls, lb.at[OWN], LBR, recv_one.at[LBR], (t + 1, r)).start()

            return local

        if early:
            image_l = applied((lb, LB))
            (image_u, b2c, gc), (image_p, b2l, gl) = applied((pu, PU, cb), (pa, PA, lb))
            known_c = (b2c, gc, below(cb, pu, b2c, gc))
            known_l = (b2l, gl, below(lb, pa, b2l, gl))
            local = finish_forcing()
        else:
            local = finish_forcing()
            pass_on(lb, LBR, LB)
            pass_on(pu, PUR, PU)
            pass_on(pa, PAR, PA)
            image_l, image_p, (image_u, b2c, gc) = applied((lb, LB), (pa, PA), (pu, PU, pa))
            known_c = (b2c, gc, below(pa, pu, b2c, gc))
        took(tp, recv_one.at[TP], parts)
        t0c, t1c, t0l, t1l, hs = unpacked(tp, 5)
        hs = hs * (1.0 / parts)
        x1, x2 = start_weights(hs, known_c, t0c, t1c)
        if early:
            x3, x4 = forcing_weights(hs, known_l, t0l, t1l)
            state = lambda p: x1 * cb[p] + x2 * pu[p] + (x3 * lb[p] + x4 * pa[p])
            image = x1 * image_c + x2 * image_u + (x3 * image_l + x4 * image_p)
        else:
            state = lambda p: x1 * pa[p] + x2 * pu[p] + lb[p]
            image = x1 * image_p + x2 * image_u + image_l
        gu[OWN] = image
        ck[OWN] = state(OWN)

        @pl.when(t + 1 < slabs)
        def _():
            relay(gu.at[OWN], pu, PUR).start()
            relay(ck.at[OWN], pa, PAR).start()

        spread(gu, GU)
        for p in range(parts):
            if p != OWN:
                ck[p] = state(p)
        own = ck[OWN]
        again, b2, g = applied((gu, GU, ck))
        tb[OWN] = packed([*sums(own, image, again, g), None, None, h])

        @pl.when(t + 1 < slabs)
        def _():
            pl.semaphore_wait(ready, 1)
            spread_next()

        spread_sums(tb, TB)
        known = (b2, g, below(ck, gu, b2, g))
        took(tb, recv_one.at[TB], last)
        x1, x2 = start_weights(h, known, *unpacked(tb, 2))
        o_ref[...] = x1 * own + x2 * image + local

    pl.when(t == 1)(functools.partial(later, True))
    pl.when(t > 1)(functools.partial(later, False))

    for buffer, k in ((fb, F), (gf, GF), (gu, GU), (tb, TB)):
        took(buffer, send.at[k], last)

    @pl.when(t < 2)
    def _():
        took(cb, send.at[C], last)

    @pl.when(t + 1 < slabs)
    def _():
        for k in (LBR, PUR, PAR):
            took(lb, send.at[k], 1)
        took(tp, send.at[TP], parts)

    @pl.when(t > 0)
    def _():
        for buffer, k in ((lb, LB), (pu, PU), (pa, PA), (tf, TF)):
            took(buffer, send.at[k], last)


def on_device(parts, slabs, coupling, damping, forcing, initial, counts):
    members, rows = initial.shape
    whole = coupling.shape[2]
    far, ram = pl.BlockSpec(memory_space=pl.ANY), pl.BlockSpec(memory_space=pltpu.SMEM)
    blocks = pltpu.VMEM((parts, members, rows), jnp.float32)
    scalars = pltpu.VMEM((parts, 1, LANES), jnp.float32)
    result = pl.pallas_call(
        functools.partial(kernel, members, rows, parts, slabs),
        out_shape=jax.ShapeDtypeStruct((members, rows), jnp.float32),
        in_specs=[far, far, far, far, ram],
        out_specs=pl.BlockSpec(memory_space=pltpu.VMEM),
        scratch_shapes=[
            pltpu.VMEM((rows, whole), jnp.float32),
            pltpu.VMEM((whole, 2 * rows), jnp.bfloat16),
            pltpu.VMEM((6 * members, whole), jnp.bfloat16),
            *[blocks] * 8,
            *[scalars] * 3,
            pltpu.VMEM((members, rows), jnp.float32),
            pltpu.VMEM((1, rows), jnp.float32),
            pltpu.SemaphoreType.DMA((CHUNKS,)),
            pltpu.SemaphoreType.DMA((3,)),
            pltpu.SemaphoreType.REGULAR,
            pltpu.SemaphoreType.DMA((13,)),
            pltpu.SemaphoreType.DMA((7, 2 * len(GROUPS))),
            pltpu.SemaphoreType.DMA((13,)),
        ],
        compiler_params=pltpu.CompilerParams(
            collective_id=0, has_side_effects=True, vmem_limit_bytes=60 << 20
        ),
    )(coupling, damping, forcing[0], initial, counts)
    return result[None]


def solution(mesh):
    placed = (P("tm", "row", None), P("tm", "row"), P("tm", None, "row"), P(None, "row"), P("tm"))
    step = functools.partial(on_device, mesh.shape["row"], mesh.shape["tm"])
    return jax.shard_map(
        step, mesh=mesh, in_specs=placed, out_specs=P("tm", None, "row"), check_vma=False
    )
```

```python
import functools
import math

import jax
import jax.numpy as jnp
from jax import lax
from jax.experimental import pallas as pl
from jax.experimental.pallas import tpu as pltpu
from jax.sharding import PartitionSpec as P

MESH = pl.DeviceIdType.MESH
TIME_STEP = 0.125
EPSILON = 1e-06
SQUARINGS = 5
TAYLOR_TERMS = 12
SIDE = 4
LANES = 128
LATE = 4
CHUNKS = 8


def steps():
    hops = lambda d: min(d, SIDE - d)
    chips = [(z, y) for z in range(SIDE) for y in range(SIDE)]
    chips.sort(key=lambda s: (-hops(s[0]) - hops(s[1]), -abs(hops(s[0]) - hops(s[1]))))
    return [(z, y, flip) for flip in (0, 1) for z, y in chips]


STEPS = steps()
CHIPS = len(STEPS) // 2
OWN = CHIPS - 1
GROUPS = ((0, 3), (3, 6), (6, 9), (9, 12), (12, 15))
BY_DISTANCE = [i + CHIPS * flip for i in range(CHIPS) for flip in (0, 1)]


def exponential(h, g, below, above, corner):
    scale = h * (1.0 / 2.0**SQUARINGS)
    s = (g * scale, above * scale, below * scale, corner * scale)
    times = lambda a, b: (
        a[0] * b[0] + a[1] * b[2], a[0] * b[1] + a[1] * b[3],
        a[2] * b[0] + a[3] * b[2], a[2] * b[1] + a[3] * b[3],
    )
    plus = lambda a, b: tuple(x + y for x, y in zip(a, b))
    s2 = times(s, s)
    s3, s4 = times(s2, s), times(s2, s2)

    def four(coefficients):
        c0, c1, c2, c3 = coefficients
        out = [(a * c1 + b * c2) + c * c3 for a, b, c in zip(s, s2, s3)]
        return (out[0] + c0, out[1], out[2], out[3] + c0)

    term = [1.0 / math.factorial(k) for k in range(TAYLOR_TERMS + 1)]
    r = plus(four(term[8:12]), tuple(x * term[12] for x in s4))
    r = plus(four(term[4:8]), times(s4, r))
    r = plus(four(term[0:4]), times(s4, r))
    edge = 1.0 / 2.0**SQUARINGS
    first = lambda a: (a[0], a[2])
    on = lambda a, v: (a[0] * v[0] + a[1] * v[1], a[2] * v[0] + a[3] * v[1])
    c = first(four(term[9:13]))
    c = plus(first(four(term[5:9])), on(s4, c))
    c = plus(first(four(term[1:5])), on(s4, c))
    c = tuple(x * edge for x in c)
    for _ in range(SQUARINGS):
        r, c = times(r, r), plus(on(r, c), c)
    return r[0], r[2], c[0], c[1]


def kernel(
    members, rows, parts, slabs,
    a_hbm, damp_hbm, f_hbm, c_hbm, n_hbm, o_ref,
    stage, at, xs, cb, fb, lb, pu, pa, gf, gu, ck, tb, tf, tp, ls, damp_ref, n_ref,
    a_sem, small_sem, ready, send, recv, recv_one,
):
    t, r = lax.axis_index("tm"), lax.axis_index("row")
    core, chip = lax.rem(r, 2), r // 2
    z, y = chip // SIDE, lax.rem(chip, SIDE)
    zs = [lax.rem(z + d, SIDE) * (2 * SIDE) for d in range(SIDE)]
    ys = [lax.rem(y + d, SIDE) * 2 for d in range(SIDE)]
    cores = (core, 1 - core)
    width = a_hbm.shape[2] // CHUNKS
    C, F, LB, PU, PA, GF, GU, LBR, PUR, PAR, TF, TB, TP = range(13)
    last = parts - 1

    def loads(j):
        return pltpu.make_async_copy(
            a_hbm.at[0, :, pl.ds(j * width, width)], stage.at[:, pl.ds(j * width, width)], a_sem.at[j]
        )

    small = [
        pltpu.make_async_copy(from_ref, to_ref, small_sem.at[i])
        for i, (from_ref, to_ref) in enumerate(
            ((f_hbm, fb.at[OWN]), (c_hbm, cb.at[OWN]), (damp_hbm, damp_ref), (n_hbm, n_ref))
        )
    ]

    def copy(src, dst, k, arrival, device):
        return pltpu.make_async_remote_copy(
            src_ref=src, dst_ref=dst, send_sem=send.at[k], recv_sem=arrival,
            device_id=device, device_id_type=MESH,
        )

    def device(i):
        dz, dy, flip = STEPS[i]
        return zs[dz] + ys[dy] + cores[flip]

    def relay(src, dst, k):
        return copy(src, dst.at[OWN], k, recv_one.at[k], (t + 1, r))

    def spread(buffer, k):
        own = buffer.at[OWN]
        for group, (low, high) in enumerate(GROUPS):
            for i in range(low, high):
                copy(own, buffer.at[i], k, recv.at[k, group], (t, device(i))).start()
        copy(own, buffer.at[last], k, recv.at[k, 2 * len(GROUPS) - 1], (t, device(last))).start()

    def forward(buffer, k):
        for group, (low, high) in enumerate(GROUPS):
            took(buffer, recv.at[k, group], high - low)
            copy(
                buffer.at[pl.ds(low, high - low)], buffer.at[pl.ds(CHIPS + low, high - low)],
                k, recv.at[k, len(GROUPS) + group], (t, device(last)),
            ).start()

    def spread_sums(buffer, k):
        for i in BY_DISTANCE:
            if i != OWN:
                copy(buffer.at[OWN], buffer.at[i], k, recv_one.at[k], (t, device(i))).start()

    def spread_next():
        for i in BY_DISTANCE:
            copy(tb.at[OWN], tp.at[i], TP, recv_one.at[TP], (t + 1, device(i))).start()

    def took(buffer, semaphore, count):
        some = buffer.at[pl.ds(0, count)]
        pltpu.make_async_copy(some, some, semaphore).wait()

    def all_left(first, second):
        for buffer, k in ((fb, F), (gf, GF), (gu, GU), (tb, TB)):
            took(buffer, send.at[k], last)
        if first or second:
            took(cb, send.at[C], last)
        if not first:
            for buffer, k in ((lb, LB), (pu, PU), (pa, PA), (tf, TF)):
                took(buffer, send.at[k], last)

        @pl.when(t + 1 < slabs)
        def _():
            for k in (LBR, PUR, PAR):
                took(lb, send.at[k], 1)
            took(tp, send.at[TP], parts)

    def fill(slot, at_part, v):
        high = v.astype(jnp.bfloat16).astype(jnp.float32)
        both = jnp.concatenate([high, v - high], axis=0).astype(jnp.bfloat16)
        xs[16 * slot : 16 * slot + 16, rows * at_part : rows * at_part + rows] = both

    def applied(*gathers, forwarded=False, then=None):
        count = len(gathers)
        total = jnp.zeros((2 * members * count, 2 * rows), jnp.float32)
        norms, d = {}, {}
        for j, (buffer, k, *beside) in enumerate(gathers):
            if not forwarded:
                forward(buffer, k)
            if beside:
                n2 = jnp.zeros((members, rows), jnp.float32)
                d[j] = jnp.zeros((members, rows), jnp.float32)
                if not any(beside[0] is earlier[0] for earlier in gathers):
                    for p in range(parts):
                        n2 += beside[0][p] * beside[0][p]
                norms[j] = n2
        ends = [0, CHIPS, *(CHIPS + high for _, high in GROUPS[:-1]), parts]
        for group, (low, high) in enumerate(zip(ends, ends[1:])):
            for j, (buffer, k, *_) in enumerate(gathers):
                if group > 0:
                    took(buffer, recv.at[k, len(GROUPS) + group - 1], high - low)
                for p in range(low, high):
                    fill(j, p, buffer[p])
            for j, (buffer, _, *beside) in enumerate(gathers):
                if beside:
                    for p in range(low, high):
                        d[j] += beside[0][p] * buffer[p]
                        if any(beside[0] is earlier[0] for earlier in gathers):
                            norms[j] += beside[0][p] * beside[0][p]
            total += jnp.dot(
                xs[0 : 16 * count, rows * low : rows * high], at[rows * low : rows * high, :],
                preferred_element_type=jnp.float32,
            )
            if group == 0 and then is not None:
                then()
        out = []
        for j, (buffer, _, *beside) in enumerate(gathers):
            at_row = 2 * members * j
            top, under = total[at_row : at_row + members], total[at_row + members : at_row + 2 * members]
            image = top[:, :rows] + (top[:, rows:] + under[:, :rows]) - damp * buffer[OWN]
            if beside:
                b2 = jnp.sum(norms[j], axis=1, keepdims=True) + EPSILON
                out.append((image, b2, jnp.sum(d[j], axis=1, keepdims=True) / b2))
            else:
                out.append(image)
        return out[0] if count == 1 else out

    def below(first, second, b2, g):
        w2 = jnp.zeros((members, rows), jnp.float32)
        for p in range(parts):
            w = second[p] - g * first[p]
            w2 += w * w
        side = jnp.sqrt(jnp.sum(w2, axis=1, keepdims=True) / b2 + EPSILON)
        inverse = 1.0 / side
        return g, side, inverse, inverse / b2

    def sums(first, second, image, g):
        w = second - g * first
        image = image - g * second
        return (
            jnp.sum(first * image, axis=1, keepdims=True),
            jnp.sum(w * image, axis=1, keepdims=True),
        )

    lane = lax.broadcasted_iota(jnp.int32, (members, LANES), 1)
    member = lax.broadcasted_iota(jnp.int32, (members, LANES), 0)

    def packed(columns):
        row = jnp.zeros((members, LANES), jnp.float32)
        for j, column in enumerate(columns):
            if column is not None:
                row = jnp.where(lane == member + members * j, column, row)
        return jnp.sum(row, axis=0, keepdims=True)

    def unpacked(buffer, count):
        parts_of = [buffer[p] for p in range(parts)]
        while len(parts_of) > 1:
            parts_of = [a + b for a, b in zip(parts_of[::2], parts_of[1::2])]
        total = jnp.broadcast_to(parts_of[0], (members, LANES))
        return [
            jnp.sum(jnp.where(lane == member + members * j, total, 0.0), axis=1, keepdims=True)
            for j in range(count)
        ]

    def start_weights(h, known, t0, t1):
        g, side, inverse, unit = known
        e00, e10, _, _ = exponential(h, g, side, t0 * unit, (t1 * unit) * inverse)
        x2 = e10 * inverse
        return e00 - g * x2, x2

    def forcing_weights(h, known, t0, t1):
        g, side, inverse, unit = known
        _, _, c0, c1 = exponential(h, g, side, t0 * unit, (t1 * unit) * inverse)
        x4 = h * c1 * inverse
        return h * c0 - g * x4, x4

    barrier = pltpu.get_barrier_semaphore()
    for i in (*range(OWN), last):
        pl.semaphore_signal(barrier, inc=1, device_id=(t, device(i)), device_id_type=MESH)

    @pl.when(t > 0)
    def _():
        pl.semaphore_signal(barrier, inc=1, device_id=(t - 1, r), device_id_type=MESH)

    @pl.when(t + 1 < slabs)
    def _():
        pl.semaphore_signal(barrier, inc=1, device_id=(t + 1, r), device_id_type=MESH)

    for copy_in in small:
        copy_in.start()
    for j in range(CHUNKS):
        loads(j).start()

    for copy_in in small:
        copy_in.wait()
    h = jnp.full((members, 1), n_ref[0].astype(jnp.float32) * TIME_STEP, jnp.float32)
    damp = damp_ref[...]
    pl.semaphore_wait(barrier, CHIPS + jnp.minimum(t, 1) + jnp.minimum(slabs - 1 - t, 1))

    @pl.when(t == 0)
    def _():
        relay(fb.at[OWN], lb, LBR).start()
        spread(cb, C)

    spread(fb, F)

    @pl.when(t == 1)
    def _():
        spread(cb, C)

    for j in range(CHUNKS):
        loads(j).wait()

    def convert(i):
        dz, dy, flip = STEPS[i]
        source = zs[(SIDE - dz) % SIDE] + ys[(SIDE - dy) % SIDE] + cores[flip]
        block = stage[:, pl.ds(pl.multiple_of(source * rows, rows), rows)].T
        high = block.astype(jnp.bfloat16)
        at[i * rows : (i + 1) * rows, 0:rows] = high
        at[i * rows : (i + 1) * rows, rows : 2 * rows] = (block - high.astype(jnp.float32)).astype(
            jnp.bfloat16
        )

    for i in range(parts - LATE):
        convert(i)

    @pl.when(t == 0)
    def _():
        forward(cb, C)

    @pl.when(t > 0)
    def _():
        forward(fb, F)

    for i in range(parts - LATE, parts):
        convert(i)

    own_f = fb[OWN]

    @pl.when(t == 0)
    def _():
        own_c = cb[OWN]
        image_c = applied((cb, C), forwarded=True, then=lambda: forward(fb, F))
        gu[OWN] = image_c
        relay(gu.at[OWN], pu, PUR).start()
        spread(gu, GU)
        image_f = applied((fb, F), forwarded=True)
        gf[OWN] = image_f
        relay(gf.at[OWN], pa, PAR).start()
        spread(gf, GF)
        image, b2, g = applied((gu, GU, cb))
        t0c, t1c = sums(own_c, image_c, image, g)
        known_c = below(cb, gu, b2, g)
        image, b2, g = applied((gf, GF, fb))
        t0f, t1f = sums(own_f, image_f, image, g)
        tb[OWN] = packed([t0c, t1c, t0f, t1f, h])
        pl.semaphore_wait(ready, 1)
        spread_next()
        spread_sums(tb, TB)
        known_f = below(fb, gf, b2, g)
        all_left(True, False)
        took(tb, recv_one.at[TB], last)
        t0c, t1c, t0f, t1f = unpacked(tb, 4)
        x1, x2 = start_weights(h, known_c, t0c, t1c)
        x3, x4 = forcing_weights(h, known_f, t0f, t1f)
        o_ref[...] = x1 * own_c + x2 * image_c + (x3 * own_f + x4 * image_f)

    def later(early):
        def pass_on(buffer, one, k):
            copy(ls, buffer.at[OWN], k, recv_one.at[one], (t, r)).wait_recv()
            spread(buffer, k)

        if early:
            pass_on(lb, LBR, LB)
        image_f = applied((fb, F), forwarded=True, then=(lambda: forward(cb, C)) if early else None)
        pl.semaphore_signal(ready, inc=1, device_id=(t - 1, r), device_id_type=MESH)
        gf[OWN] = image_f
        spread(gf, GF)
        if early:
            image_c = applied((cb, C), forwarded=True)
            pass_on(pu, PUR, PU)
            pass_on(pa, PAR, PA)
        image, b2, g = applied((gf, GF, fb))
        tf[OWN] = packed(list(sums(own_f, image_f, image, g)))
        spread_sums(tf, TF)
        known_f = below(fb, gf, b2, g)

        def finish_forcing():
            took(tf, recv_one.at[TF], last)
            x3, x4 = forcing_weights(h, known_f, *unpacked(tf, 2))
            local = x3 * own_f + x4 * image_f

            @pl.when(t + 1 < slabs)
            def _():
                ls[...] = local
                copy(ls, lb.at[OWN], LBR, recv_one.at[LBR], (t + 1, r)).start()

            return local

        if early:
            image_l = applied((lb, LB))
            (image_u, b2c, gc), (image_p, b2l, gl) = applied((pu, PU, cb), (pa, PA, lb))
            known_c = below(cb, pu, b2c, gc)
            known_l = below(lb, pa, b2l, gl)
            local = finish_forcing()
        else:
            local = finish_forcing()
            pass_on(lb, LBR, LB)
            pass_on(pu, PUR, PU)
            pass_on(pa, PAR, PA)
            image_l, image_p, (image_u, b2c, gc) = applied((lb, LB), (pa, PA), (pu, PU, pa))
            known_c = below(pa, pu, b2c, gc)
        took(tp, recv_one.at[TP], parts)
        t0c, t1c, t0l, t1l, hs = unpacked(tp, 5)
        hs = hs * (1.0 / parts)
        x1, x2 = start_weights(hs, known_c, t0c, t1c)
        if early:
            x3, x4 = forcing_weights(hs, known_l, t0l, t1l)
            state = lambda p: x1 * cb[p] + x2 * pu[p] + (x3 * lb[p] + x4 * pa[p])
            image = x1 * image_c + x2 * image_u + (x3 * image_l + x4 * image_p)
        else:
            state = lambda p: x1 * pa[p] + x2 * pu[p] + lb[p]
            image = x1 * image_p + x2 * image_u + image_l
        gu[OWN] = image
        ck[OWN] = state(OWN)

        @pl.when(t + 1 < slabs)
        def _():
            relay(gu.at[OWN], pu, PUR).start()
            relay(ck.at[OWN], pa, PAR).start()

        spread(gu, GU)
        for p in range(parts):
            if p != OWN:
                ck[p] = state(p)
        own = ck[OWN]
        again, b2, g = applied((gu, GU, ck))
        tb[OWN] = packed([*sums(own, image, again, g), None, None, h])

        @pl.when(t + 1 < slabs)
        def _():
            pl.semaphore_wait(ready, 1)
            spread_next()

        spread_sums(tb, TB)
        known = below(ck, gu, b2, g)
        all_left(False, early)
        took(tb, recv_one.at[TB], last)
        x1, x2 = start_weights(h, known, *unpacked(tb, 2))
        o_ref[...] = x1 * own + x2 * image + local

    pl.when(t == 1)(functools.partial(later, True))
    pl.when(t > 1)(functools.partial(later, False))


def on_device(parts, slabs, coupling, damping, forcing, initial, counts):
    members, rows = initial.shape
    whole = coupling.shape[2]
    far = pl.BlockSpec(memory_space=pl.ANY)
    blocks = pltpu.VMEM((parts, members, rows), jnp.float32)
    scalars = pltpu.VMEM((parts, 1, LANES), jnp.float32)
    result = pl.pallas_call(
        functools.partial(kernel, members, rows, parts, slabs),
        out_shape=jax.ShapeDtypeStruct((members, rows), jnp.float32),
        in_specs=[far] * 5,
        out_specs=pl.BlockSpec(memory_space=pltpu.VMEM),
        scratch_shapes=[
            pltpu.VMEM((rows, whole), jnp.float32),
            pltpu.VMEM((whole, 2 * rows), jnp.bfloat16),
            pltpu.VMEM((6 * members, whole), jnp.bfloat16),
            *[blocks] * 8,
            *[scalars] * 3,
            pltpu.VMEM((members, rows), jnp.float32),
            pltpu.VMEM((1, rows), jnp.float32),
            pltpu.SMEM((1,), jnp.int32),
            pltpu.SemaphoreType.DMA((CHUNKS,)),
            pltpu.SemaphoreType.DMA((4,)),
            pltpu.SemaphoreType.REGULAR,
            pltpu.SemaphoreType.DMA((13,)),
            pltpu.SemaphoreType.DMA((7, 2 * len(GROUPS))),
            pltpu.SemaphoreType.DMA((13,)),
        ],
        compiler_params=pltpu.CompilerParams(
            collective_id=0, has_side_effects=True, vmem_limit_bytes=60 << 20
        ),
    )(coupling, damping, forcing[0], initial, counts)
    return result[None]


def solution(mesh):
    placed = (P("tm", "row", None), P("tm", "row"), P("tm", None, "row"), P(None, "row"), P("tm"))
    step = functools.partial(on_device, mesh.shape["row"], mesh.shape["tm"])
    return jax.shard_map(
        step, mesh=mesh, in_specs=placed, out_specs=P("tm", None, "row"), check_vma=False
    )
```
